512 devices in a mesh: row: 16 (over y, z_hi, core), col: 32 (over z_lo, x).
Axes of the slice: x: 4, y: 4, z: 16 (z_hi: 2, z_lo: 8; z = z_hi * 8 + z_lo), core: 2. Of those that a mesh axis runs over, the one named last changes fastest.
Arguments:
- pair_features: bfloat16 [64, 2048, 2048], P(None, 'col', 'row'), may hold values from -6 to 6
- first_block_kernel: bfloat16 [3, 3, 64, 64], replicated, may hold values from -0.25 to 0.25
- first_block_bias: float32 [64], replicated, may hold values from -3 to 3
- second_block_kernel: bfloat16 [3, 3, 64, 64], replicated, may hold values from -0.25 to 0.25
- second_block_bias: float32 [64], replicated, may hold values from -3 to 3
- head_weight: bfloat16 [37, 64], replicated, may hold values from -32 to 32
- head_bias: float32 [37], replicated, may hold values from -4 to 4
- target: int32 [2048, 2048], P('col', 'row'), may hold values from 0 to 36
Outputs:
- feat_grad: float32 [64, 2048, 2048], P(None, 'col', 'row')
The draws below stay inside these ranges and needn't reach their ends.
All inputs are finite; a program needn't handle non-finite values.
Results may differ from the reference program's by a relative error of at most 0.0055.
The reference program's roundings to bfloat16 on the way count: a program that leaves them out, or rounds other values in their place, can miss the bound.
Values may be sent and summed in bfloat16 or wider, within the bound.
A program may use at most 64 MiB of HBM per device.

```python
import math
import jax
import jax.numpy as jnp
from jax import lax

C = 64
NB = 37
DILATION_FIRST = 4
DILATION_SECOND = 8
RESIDUES = 2048


def draw_head_weight(key, part):
    key_main = jax.random.fold_in(key, 0)
    gaussian = jax.random.normal(key_main, (NB, C), jnp.float32)
    scaled = 3.0 / math.sqrt(C) * gaussian
    return jnp.clip(scaled, -32.0, 32.0).astype(jnp.bfloat16)


def set_ends(entries, rng, least, largest):
    index_at = [jax.random.randint(jax.random.fold_in(rng, axis), (), 0, length) for axis, length in enumerate(entries.shape)]
    main_axis = entries.shape.index(max(entries.shape))
    next_to = index_at[:main_axis] + [(index_at[main_axis] + 1) % entries.shape[main_axis]] + index_at[main_axis + 1:]
    return entries.at[tuple(index_at)].set(least).at[tuple(next_to)].set(largest)


def levels(own_key, dims, pieces, low, top_value):
    level = 1.0
    for dim, parts in pieces:
        draws = jax.random.uniform(jax.random.fold_in(jax.random.fold_in(own_key, 6), dim), (parts,), jnp.float32, low / len(pieces), top_value / len(pieces))
        level = level * jnp.repeat(jnp.exp(draws), dims[dim] // parts).reshape((-1,) + (1,) * (len(dims) - 1 - dim))
    return level


def noise(own_key, shape, deviation, limit, shards=(), kind=jnp.bfloat16):
    values = deviation * jax.random.normal(own_key, shape, jnp.float32)
    if shards:
        values = values * levels(own_key, shape, shards, -0.22, 0.18)
    return jnp.clip(values, -limit, limit).astype(kind)


def setup_inputs(seed: int = 0) -> dict:
    splits = jax.random.split(jax.random.key(seed), 9)
    return {
        "pair_features": noise(splits[0], (C, RESIDUES, RESIDUES), 1.0, 6.0, ((1, 32), (2, 16))),
        "first_block_kernel": noise(splits[1], (3, 3, C, C), (9 * C) ** -0.5, 0.25),
        "first_block_bias": noise(splits[2], (C,), 0.5, 3.0, (), jnp.float32),
        "second_block_kernel": noise(splits[3], (3, 3, C, C), (9 * C) ** -0.5, 0.25),
        "second_block_bias": noise(splits[4], (C,), 0.5, 3.0, (), jnp.float32),
        "head_weight": draw_head_weight(jax.random.fold_in(splits[8], 71), 0),
        "head_bias": noise(splits[6], (NB,), 1.0, 4.0, (), jnp.float32),
        "target": set_ends(jax.random.randint(splits[7], (RESIDUES, RESIDUES), 0, NB), jax.random.fold_in(splits[7], 1), 0, NB - 1).astype(jnp.int32),
    }


def rounded(tensor):
    return lax.optimization_barrier(tensor.astype(jnp.bfloat16))


def activate(pre_act):
    return jnp.where(pre_act > 0, pre_act, jnp.exp(jnp.minimum(pre_act, 0.0)) - 1.0)


def slope(pre_act):
    return jnp.where(pre_act > 0, 1.0, jnp.exp(jnp.minimum(pre_act, 0.0)))


def flipped_kernel(kernel):
    return jnp.transpose(kernel[::-1, ::-1], (0, 1, 3, 2))


def dilated_kernel(source, kernel, spacing):
    channels, first_len, second_len = source.shape
    padded_input = jnp.pad(source, ((0, 0), (spacing, spacing), (spacing, spacing)))
    summed = jnp.zeros((kernel.shape[2], first_len * second_len), jnp.float32)
    for tap_first in range(3):
        for tap_second in range(3):
            window = padded_input[:, tap_first * spacing:tap_first * spacing + first_len, tap_second * spacing:tap_second * spacing + second_len]
            summed = summed + jnp.dot(kernel[tap_first, tap_second], window.reshape(channels, -1), preferred_element_type=jnp.float32)
    return summed.reshape(kernel.shape[2], first_len, second_len)


def reference(pair_features, first_block_kernel, first_block_bias, second_block_kernel, second_block_bias, head_weight, head_bias, target):
    channels, first_len, second_len = pair_features.shape
    first_preactivation = pair_features.astype(jnp.float32) + dilated_kernel(pair_features, first_block_kernel, DILATION_FIRST) + first_block_bias[:, None, None]
    first_hidden = rounded(activate(first_preactivation))
    second_preactivation = first_hidden.astype(jnp.float32) + dilated_kernel(first_hidden, second_block_kernel, DILATION_SECOND) + second_block_bias[:, None, None]
    hidden_two = rounded(activate(second_preactivation))
    mirrored = jnp.swapaxes(hidden_two, 1, 2)
    symmetric = rounded(hidden_two.astype(jnp.float32) + mirrored.astype(jnp.float32))
    logits = jnp.dot(head_weight, symmetric.reshape(channels, -1), preferred_element_type=jnp.float32) + head_bias[:, None]
    probability = jax.nn.softmax(logits, axis=0)
    labels = (jnp.arange(NB, dtype=jnp.int32)[:, None] == target.reshape(1, -1)).astype(jnp.float32)
    grad_bins = rounded(probability - labels).reshape(NB, first_len, second_len)
    bins_sum = rounded(grad_bins.astype(jnp.float32) + jnp.swapaxes(grad_bins, 1, 2).astype(jnp.float32))
    grad_two = jnp.dot(head_weight.T, bins_sum.reshape(NB, -1), preferred_element_type=jnp.float32).reshape(channels, first_len, second_len)
    second_delta = rounded(grad_two * slope(second_preactivation))
    first_gradient = second_delta.astype(jnp.float32) + dilated_kernel(second_delta, flipped_kernel(second_block_kernel), DILATION_SECOND)
    first_delta = rounded(first_gradient * slope(first_preactivation))
    return first_delta.astype(jnp.float32) + dilated_kernel(first_delta, flipped_kernel(first_block_kernel), DILATION_FIRST)
```

```python
import functools

import jax
import jax.numpy as jnp
from jax import lax
from jax.experimental import pallas as pl
from jax.experimental.pallas import tpu as pltpu
from jax.sharding import PartitionSpec as P

D1 = 4
D2 = 8
HALO = D1 + D2
PER = 128 // HALO
MESH = pl.DeviceIdType.MESH
F32, BF16 = jnp.float32, jnp.bfloat16


def kernel(
    rows, cols, x_hbm, w1, w1t, w2, w2t, b1, b2, hw, hwt, hb, target, out,
    xm, xh, hm, hh, dm, dh, em, eh, ybuf, slope1, slope2, hid, turned,
    pack_out, pack_in, mir_out, mir_in, tgt_out, tgt_in, tgt_here, send, recv, local,
):
    r, c = lax.axis_index("row"), lax.axis_index("col")
    tp, ch, tq = out.shape
    half = tp // 2
    ext = tp + 2 * HALO
    blocks = pack_in.shape[2]
    up, down, left, right = c > 0, c < cols - 1, r > 0, r < rows - 1
    at_up, at_down = (r, jnp.maximum(c - 1, 0)), (r, jnp.minimum(c + 1, cols - 1))
    at_left, at_right = (jnp.maximum(r - 1, 0), c), (jnp.minimum(r + 1, rows - 1), c)
    partners = [(c // 2, 2 * r), (c // 2, 2 * r + 1)]
    other = [jnp.logical_or(pr != r, pc != c) for pr, pc in partners]
    mine = c % 2

    load = pltpu.make_async_copy(x_hbm, xm.at[pl.ds(HALO, tp)], local.at[0])
    load.start()

    barrier = pltpu.get_barrier_semaphore()
    friends = [(up, at_up), (down, at_down), (left, at_left), (right, at_right)]
    friends += list(zip(other, partners))
    for there, who in friends:
        @pl.when(there)
        def _(who=who):
            pl.semaphore_signal(barrier, inc=1, device_id=who, device_id_type=MESH)
    pl.semaphore_wait(barrier, sum(there.astype(jnp.int32) for there, _ in friends))

    lane = lax.broadcasted_iota(jnp.int32, (ch, tq), 1)
    low = lane < tq // 2

    def remote(src, dst, k, who, k_there=None):
        return pltpu.make_async_remote_copy(
            src_ref=src, dst_ref=dst, send_sem=send.at[k],
            recv_sem=recv.at[k if k_there is None else k_there],
            device_id=who, device_id_type=MESH,
        )

    whole = target[...].astype(F32)
    whole = jnp.transpose(jnp.concatenate([whole, whole], axis=0))
    low_rows = lax.broadcasted_iota(jnp.int32, (half, tq), 1) < tq // 2
    for h in range(2):
        a = whole[tp * h : tp * h + half]
        b = whole[tp * h + half : tp * (h + 1)]
        tgt_out[h] = jnp.where(low_rows, a, b)
    def swap(src, dst, k):
        outgoing = [
            remote(src.at[h], dst.at[mine], k + h, partners[h], k + mine) for h in range(2)
        ]
        incoming = [remote(src.at[g], dst.at[g], k + g, partners[g]) for g in range(2)]
        for h in range(2):
            @pl.when(other[h])
            def _(h=h):
                outgoing[h].start()

            @pl.when(jnp.logical_not(other[h]))
            def _(h=h):
                dst[h] = src[h]

        def arrive():
            for g in range(2):
                @pl.when(other[g])
                def _(g=g):
                    incoming[g].wait_recv()

        def leave():
            for h in range(2):
                @pl.when(other[h])
                def _(h=h):
                    outgoing[h].wait_send()

        return arrive, leave

    tgt_arrive, tgt_leave = swap(tgt_out, tgt_in, 16)

    def edges(main, halo, which, base):
        first = remote(main.at[pl.ds(HALO, HALO)], main.at[pl.ds(HALO + tp, HALO)], base, at_up)
        last = remote(main.at[pl.ds(tp, HALO)], main.at[pl.ds(0, HALO)], base + 1, at_down)
        parts = [(2, blocks - 4), (0, 2), (blocks - 2, 2)]

        def side(s, n):
            lo, count = parts[n]
            span = pl.ds(lo, count)
            return remote(
                pack_out.at[which, s, span], pack_in.at[which, s, span],
                base + 2 + 3 * s + n, (at_left, at_right)[s],
            )

        @pl.when(up)
        def _():
            first.start()

        @pl.when(down)
        def _():
            last.start()

        def pack(b, carry):
            first_lanes = jnp.zeros((ch, tq), F32)
            last_lanes = jnp.zeros((ch, tq), F32)
            for j in range(PER):
                row = main[b * PER + j].astype(F32)
                slot = jnp.logical_and(lane >= HALO * j, lane < HALO * (j + 1))
                shifted = pltpu.roll(row, HALO * j, 1) if j else row
                first_lanes = jnp.where(slot, shifted, first_lanes)
                last_lanes = jnp.where(
                    slot, pltpu.roll(row, (HALO * (j + 1)) % tq, 1), last_lanes
                )
            pack_out[which, 0, b] = first_lanes.astype(BF16)
            pack_out[which, 1, b] = last_lanes.astype(BF16)
            return carry

        def begin(n):
            @pl.when(left)
            def _():
                side(0, n).start()

            @pl.when(right)
            def _():
                side(1, n).start()

        lax.fori_loop(2, blocks - 2, pack, 0)
        begin(0)

        @pl.when(down)
        def _():
            first.wait_recv()

        @pl.when(jnp.logical_not(down))
        def _():
            main[pl.ds(HALO + tp, HALO)] = jnp.zeros((HALO, ch, tq), BF16)

        @pl.when(up)
        def _():
            last.wait_recv()

        @pl.when(jnp.logical_not(up))
        def _():
            main[pl.ds(0, HALO)] = jnp.zeros((HALO, ch, tq), BF16)

        lax.fori_loop(0, 2, pack, 0)
        begin(1)
        lax.fori_loop(blocks - 2, blocks, pack, 0)
        begin(2)

        for n in range(3):
            @pl.when(right)
            def _(n=n):
                side(0, n).wait_recv()

            @pl.when(left)
            def _(n=n):
                side(1, n).wait_recv()

        for s, there in ((0, right), (1, left)):
            @pl.when(jnp.logical_not(there))
            def _(s=s):
                pack_in[which, s] = jnp.zeros(pack_in.shape[2:], BF16)

        def unpack(b, carry):
            after = pack_in[which, 0, b].astype(F32)
            before = pack_in[which, 1, b].astype(F32)
            for j in range(PER):
                a = pltpu.roll(after, (-HALO * j) % tq, 1) if j else after
                z = pltpu.roll(before, (-HALO * (j + 1)) % tq, 1)
                halo[b * PER + j] = jnp.where(low, a, z).astype(BF16)
            return carry

        lax.fori_loop(0, blocks, unpack, 0)

        def finish():
            @pl.when(up)
            def _():
                first.wait_send()

            @pl.when(down)
            def _():
                last.wait_send()

            for n in range(3):
                @pl.when(left)
                def _(n=n):
                    side(0, n).wait_send()

                @pl.when(right)
                def _(n=n):
                    side(1, n).wait_send()

        return finish

    def taps(main, halo, d, wide):
        lm, lh = pltpu.roll(main, tq - d, 1), pltpu.roll(halo, tq - d, 1)
        rm, rh = pltpu.roll(main, d, 1), pltpu.roll(halo, d, 1)
        head, tail = lane < d, lane >= tq - d
        first = [jnp.where(head, rh, rm), main, jnp.where(tail, lh, lm)]
        first = jnp.concatenate(first, axis=0).astype(BF16)
        if not wide:
            return first
        second = [jnp.where(head, rm, rh), halo, jnp.where(tail, lm, lh)]
        return jnp.concatenate([first, jnp.concatenate(second, axis=0).astype(BF16)], axis=1)

    def conv(weights, patches, count, lag, done):
        w = weights[...]

        def step(j, finish):
            y = jnp.dot(w, patches(j), preferred_element_type=F32)
            ybuf[j] = y[: 2 * ch]
            if finish:
                done(j - 2 * lag, ybuf[j - 2 * lag, :ch] + ybuf[j - lag, ch:] + y[2 * ch :])

        def loop(lo, hi, finish):
            def body(j, carry):
                step(lo + 2 * j, finish)
                step(lo + 2 * j + 1, finish)
                return carry

            lax.fori_loop(0, (hi - lo) // 2, body, 0)

        loop(0, 2 * lag, False)
        loop(2 * lag, count, True)

    def wide_rows(main, halo, d):
        return lambda j: taps(main[j].astype(F32), halo[j].astype(F32), d, True)

    def row_pairs(main, halo, d):
        def patches(j):
            one = taps(main[2 * j].astype(F32), halo[2 * j].astype(F32), d, False)
            two = taps(main[2 * j + 1].astype(F32), halo[2 * j + 1].astype(F32), d, False)
            return jnp.concatenate([one, two], axis=1)

        return patches

    side_ok = jnp.where(low, jnp.where(right, 1.0, 0.0), jnp.where(left, 1.0, 0.0))

    def row_ok(p):
        inside = jnp.logical_and(jnp.logical_or(up, p >= 0), jnp.logical_or(down, p < tp))
        return jnp.where(inside, 1.0, 0.0).astype(F32)

    load.wait()
    pad = blocks * PER - ext
    if pad:
        xm[pl.ds(ext, pad)] = jnp.zeros((pad, ch, tq), BF16)
        dm[pl.ds(ext, pad)] = jnp.zeros((pad, ch, tq), BF16)
    finish_x = edges(xm, xh, 0, 0)
    bias1 = jnp.broadcast_to(b1[...], (ch, tq))
    bias2 = jnp.broadcast_to(b2[...], (ch, tq))

    def first_done(o, total):
        ok = row_ok(o - D2)
        for n, (src, dst) in enumerate(((xm, hm), (xh, hh))):
            pre = src[o + D1].astype(F32) + total[:, tq * n : tq * (n + 1)] + bias1
            e = jnp.exp(jnp.minimum(pre, 0.0))
            slope1[o, :, tq * n : tq * (n + 1)] = jnp.where(pre > 0, 1.0, e)
            act = jnp.where(pre > 0, pre, e - 1.0) * ok
            dst[o] = (act * side_ok if n else act).astype(BF16)

    conv(w1, wide_rows(xm, xh, D1), ext, D1, first_done)

    def second_done(m, total):
        for n in range(2):
            o = 2 * m + n
            pre = hm[o + D2].astype(F32) + total[:, tq * n : tq * (n + 1)] + bias2
            e = jnp.exp(jnp.minimum(pre, 0.0))
            slope2[o] = jnp.where(pre > 0, 1.0, e)
            hid[o] = jnp.where(pre > 0, pre, e - 1.0).astype(BF16).astype(F32)

    conv(w2, row_pairs(hm, hh, D2), (tp + 2 * D2) // 2, D2 // 2, second_done)

    def turn(o, carry):
        plane = hid[:, o, :]
        plane = jnp.transpose(jnp.concatenate([plane, plane], axis=0))
        for h in range(2):
            a = plane[tp * h : tp * h + half]
            b = plane[tp * h + half : tp * (h + 1)]
            turned[pl.ds(half * h, half), o, :] = jnp.where(low_rows, a, b)
        return carry

    lax.fori_loop(0, ch, turn, 0)

    def settle(j, carry):
        mir_out[0, j] = turned[j].astype(BF16)
        mir_out[1, j] = turned[half + j].astype(BF16)
        return carry

    lax.fori_loop(0, half, settle, 0)

    mir_arrive, mir_leave = swap(mir_out, mir_in, 18)
    tgt_arrive()
    mir_arrive()

    weight, weight_t = hw[...], hwt[...]
    bins = weight.shape[0]
    bias = jnp.broadcast_to(hb[...], (bins, 2 * tq))
    bin_ids = lax.broadcasted_iota(jnp.int32, (bins, 2 * tq), 0).astype(F32)
    low_row = lax.broadcasted_iota(jnp.int32, (1, tq), 1) < tq // 2

    def facing(zero, one, mask):
        first = jnp.where(mask, zero, pltpu.roll(one, tq // 2, 1))
        second = jnp.where(mask, pltpu.roll(zero, tq // 2, 1), one)
        return jnp.concatenate([first, second], axis=1)

    tgt_here[...] = target[...].astype(F32)

    def head(j, carry):
        mirrored = facing(mir_in[0, j].astype(F32), mir_in[1, j].astype(F32), low)
        own = jnp.concatenate([hid[j], hid[j + half]], axis=1)
        symmetric = (own + mirrored).astype(BF16)
        logits = jnp.dot(weight, symmetric, preferred_element_type=F32) + bias
        e = jnp.exp(logits - jnp.max(logits, axis=0, keepdims=True))
        probability = e / jnp.sum(e, axis=0, keepdims=True)
        t_own = jnp.concatenate(
            [tgt_here[pl.ds(j, 1), :], tgt_here[pl.ds(j + half, 1), :]], axis=1
        )
        t_mirror = facing(tgt_in[0, pl.ds(j, 1), :], tgt_in[1, pl.ds(j, 1), :], low_row)
        grad = (probability - (bin_ids == t_own).astype(F32)).astype(BF16).astype(F32)
        grad_mirror = (probability - (bin_ids == t_mirror).astype(F32)).astype(BF16).astype(F32)
        bins_sum = (grad + grad_mirror).astype(BF16)
        back = jnp.dot(weight_t, bins_sum, preferred_element_type=F32)
        for n in range(2):
            o = j + half * n
            dm[HALO + o] = (back[:, tq * n : tq * (n + 1)] * slope2[o]).astype(BF16)
        return carry

    lax.fori_loop(0, half, head, 0)

    finish_d = edges(dm, dh, 1, 8)

    def second_back(o, total):
        ok = row_ok(o - D1)
        for n, (src, dst) in enumerate(((dm, em), (dh, eh))):
            grad = src[o + D2].astype(F32) + total[:, tq * n : tq * (n + 1)]
            delta = grad * slope1[o + D1, :, tq * n : tq * (n + 1)] * ok
            dst[o] = (delta * side_ok if n else delta).astype(BF16)

    conv(w2t, wide_rows(dm, dh, D2), ext, D2, second_back)

    def first_back(m, total):
        for n in range(2):
            o = 2 * m + n
            out[o] = em[o + D1].astype(F32) + total[:, tq * n : tq * (n + 1)]

    conv(w1t, row_pairs(em, eh, D1), (tp + 2 * D1) // 2, D1 // 2, first_back)

    tgt_leave()
    finish_x()
    mir_leave()
    finish_d()


def conv_weights(kernel):
    taps, _, outs, ins = kernel.shape
    return jnp.transpose(kernel, (0, 2, 1, 3)).reshape(taps * outs, taps * ins)


def turned_weights(kernel):
    return conv_weights(jnp.transpose(kernel[::-1, ::-1], (0, 1, 3, 2)))


def local_step(
    rows, cols, pair_features, first_kernel, first_bias, second_kernel, second_bias,
    head_weight, head_bias, target,
):
    ch, tp, tq = pair_features.shape
    bins = head_weight.shape[0]
    padded = -(-bins // 8) * 8
    ext = tp + 2 * HALO
    blocks = -(-ext // PER)
    hw = jnp.pad(head_weight, ((0, padded - bins), (0, 0)))
    hb = jnp.pad(head_bias, (0, padded - bins), constant_values=-1e30)
    vmem = pl.BlockSpec(memory_space=pltpu.VMEM)
    plane = lambda n, dtype=BF16: pltpu.VMEM((n, ch, tq), dtype)
    out = pl.pallas_call(
        functools.partial(kernel, rows, cols),
        out_shape=jax.ShapeDtypeStruct((tp, ch, tq), F32),
        in_specs=[pl.BlockSpec(memory_space=pl.ANY)] + [vmem] * 10,
        out_specs=vmem,
        scratch_shapes=[
            plane(blocks * PER), plane(blocks * PER),
            plane(tp + 2 * D2), plane(tp + 2 * D2),
            plane(blocks * PER), plane(blocks * PER),
            plane(tp + 2 * D1), plane(tp + 2 * D1),
            pltpu.VMEM((ext, 2 * ch, 2 * tq), F32),
            pltpu.VMEM((tp + 2 * D2, ch, 2 * tq), F32),
            plane(tp, F32), plane(tp, F32), plane(tp, F32),
            pltpu.VMEM((2, 2, blocks, ch, tq), BF16),
            pltpu.VMEM((2, 2, blocks, ch, tq), BF16),
            pltpu.VMEM((2, tp // 2, ch, tq), BF16),
            pltpu.VMEM((2, tp // 2, ch, tq), BF16),
            pltpu.VMEM((2, tp // 2, tq), F32),
            pltpu.VMEM((2, tp // 2, tq), F32),
            pltpu.VMEM((tp, tq), F32),
            pltpu.SemaphoreType.DMA((20,)),
            pltpu.SemaphoreType.DMA((20,)),
            pltpu.SemaphoreType.DMA((1,)),
        ],
        compiler_params=pltpu.CompilerParams(
            collective_id=0, has_side_effects=True, vmem_limit_bytes=60 * 1024 * 1024
        ),
    )(
        jnp.transpose(pair_features, (1, 0, 2)),
        conv_weights(first_kernel), turned_weights(first_kernel),
        conv_weights(second_kernel), turned_weights(second_kernel),
        first_bias[:, None], second_bias[:, None], hw, hw.T, hb[:, None], target,
    )
    return jnp.transpose(out, (1, 0, 2))


def solution(mesh):
    placed = (P(None, "col", "row"), P(), P(), P(), P(), P(), P(), P("col", "row"))
    return jax.shard_map(
        functools.partial(local_step, mesh.shape["row"], mesh.shape["col"]),
        mesh=mesh, in_specs=placed, out_specs=P(None, "col", "row"), check_vma=False,
    )
```

```python
import functools

import jax
import jax.numpy as jnp
from jax import lax
from jax.experimental import pallas as pl
from jax.experimental.pallas import tpu as pltpu
from jax.sharding import PartitionSpec as P

D1 = 4
D2 = 8
HALO = D1 + D2
PER = 128 // HALO
SPREAD = 4
HEADS = 2
MESH = pl.DeviceIdType.MESH
F32, BF16 = jnp.float32, jnp.bfloat16


def kernel(
    rows, cols, x_hbm, k1, k2, b1, b2, hw, hb, target, out,
    xm, xh, hm, hh, dm, dh, em, eh, w1, w1t, w2, w2t, slope1, slope2, hid, turned,
    pack_out, pack_in, mir_out, mir_in, relay, tgt_out, tgt_in, tgt_here, send, recv, local,
    leave_sem, enter_sem, pass_sem, land_sem, head_pad, bias_pad, *ybufs,
):
    r, c = lax.axis_index("row"), lax.axis_index("col")
    tp, ch, tq = out.shape
    half = tp // 2
    ext = tp + 2 * HALO
    blocks = pack_in.shape[2]
    up, down, left, right = c > 0, c < cols - 1, r > 0, r < rows - 1
    at_up, at_down = (r, jnp.maximum(c - 1, 0)), (r, jnp.minimum(c + 1, cols - 1))
    at_left, at_right = (jnp.maximum(r - 1, 0), c), (jnp.minimum(r + 1, rows - 1), c)
    partners = [(c // 2, 2 * r), (c // 2, 2 * r + 1)]
    mine = c % 2
    group = rows // SPREAD

    def elsewhere(who):
        return jnp.logical_or(who[0] != r, who[1] != c)

    other = [elsewhere(who) for who in partners]

    def shifted(row, d):
        return (row // group + d) % SPREAD * group + row % group

    via = [(shifted(r, d), c) for d in range(SPREAD)]
    relayed = [[(c // 2, 2 * shifted(r, SPREAD - d) + h) for h in range(2)] for d in range(SPREAD)]
    relays = [[(shifted(c // 2, d), 2 * r + g) for g in range(2)] for d in range(SPREAD)]

    load = pltpu.make_async_copy(x_hbm, xm.at[pl.ds(HALO, tp)], local.at[0])
    load.start()

    barrier = pltpu.get_barrier_semaphore()
    friends = [(up, at_up), (down, at_down), (left, at_left), (right, at_right)]
    friends += list(zip(other, partners))
    greeted = friends + [(elsewhere(who), who) for d in range(1, SPREAD) for who in relays[d]]
    friends = friends + [(elsewhere(who), who) for d in range(1, SPREAD) for who in relayed[d]]
    for d in range(1, SPREAD):
        pl.semaphore_signal(barrier, inc=1, device_id=via[d], device_id_type=MESH)
    for there, who in greeted:
        @pl.when(there)
        def _(who=who):
            pl.semaphore_signal(barrier, inc=1, device_id=who, device_id_type=MESH)
    lane = lax.broadcasted_iota(jnp.int32, (ch, tq), 1)
    low = lane < tq // 2

    def remote(src, dst, k, who, k_there=None):
        return pltpu.make_async_remote_copy(
            src_ref=src, dst_ref=dst, send_sem=send.at[k],
            recv_sem=recv.at[k if k_there is None else k_there],
            device_id=who, device_id_type=MESH,
        )

    whole = target[...].astype(F32)
    whole = jnp.transpose(jnp.concatenate([whole, whole], axis=0))
    low_rows = lax.broadcasted_iota(jnp.int32, (half, tq), 1) < tq // 2
    for h in range(2):
        a = whole[tp * h : tp * h + half]
        b = whole[tp * h + half : tp * (h + 1)]
        tgt_out[h] = jnp.where(low_rows, a, b)
    for kernel_ref, straight, turned_ref in ((k1, w1, w1t), (k2, w2, w2t)):
        for t in range(3):
            blocks_t = [kernel_ref[t, n] for n in range(3)]
            straight[pl.ds(ch * t, ch)] = jnp.concatenate(blocks_t, axis=1)
            back = [jnp.transpose(kernel_ref[2 - t, 2 - n].astype(F32)) for n in range(3)]
            turned_ref[pl.ds(ch * t, ch)] = jnp.concatenate(back, axis=1).astype(BF16)
    bias1 = jnp.transpose(jnp.broadcast_to(b1[...], (tq, ch)))
    bias2 = jnp.transpose(jnp.broadcast_to(b2[...], (tq, ch)))

    def swap(src, dst, k):
        outgoing = [
            remote(src.at[h], dst.at[mine], k + h, partners[h], k + mine) for h in range(2)
        ]
        incoming = [remote(src.at[g], dst.at[g], k + g, partners[g]) for g in range(2)]
        for h in range(2):
            @pl.when(other[h])
            def _(h=h):
                outgoing[h].start()

            @pl.when(jnp.logical_not(other[h]))
            def _(h=h):
                dst[h] = src[h]

        def arrive():
            for g in range(2):
                @pl.when(other[g])
                def _(g=g):
                    incoming[g].wait_recv()

        def leave():
            for h in range(2):
                @pl.when(other[h])
                def _(h=h):
                    outgoing[h].wait_send()

        return arrive, leave

    def edges(main, halo, which, base, ready):
        first = remote(main.at[pl.ds(HALO, HALO)], main.at[pl.ds(HALO + tp, HALO)], base, at_up)
        last = remote(main.at[pl.ds(tp, HALO)], main.at[pl.ds(0, HALO)], base + 1, at_down)
        parts = [(2, blocks - 4), (0, 2), (blocks - 2, 2)]

        def side(s, n):
            lo, count = parts[n]
            span = pl.ds(lo, count)
            return remote(
                pack_out.at[which, s, span], pack_in.at[which, s, span],
                base + 2 + 3 * s + n, (at_left, at_right)[s],
            )

        def pack(b, carry):
            first_lanes = jnp.zeros((ch, tq), BF16)
            last_lanes = jnp.zeros((ch, tq), BF16)
            for j in range(PER):
                row = main[b * PER + j]
                slot = jnp.logical_and(lane >= HALO * j, lane < HALO * (j + 1))
                moved = pltpu.roll(row, HALO * j, 1) if j else row
                first_lanes = jnp.where(slot, moved, first_lanes)
                last_lanes = jnp.where(
                    slot, pltpu.roll(row, HALO * (j + 1), 1), last_lanes
                )
            pack_out[which, 0, b] = first_lanes
            pack_out[which, 1, b] = last_lanes
            return carry

        def begin(n):
            @pl.when(left)
            def _():
                side(0, n).start()

            @pl.when(right)
            def _():
                side(1, n).start()

        lax.fori_loop(2, blocks - 2, pack, 0)
        ready()

        @pl.when(up)
        def _():
            first.start()

        @pl.when(down)
        def _():
            last.start()

        begin(0)

        @pl.when(down)
        def _():
            first.wait_recv()

        @pl.when(jnp.logical_not(down))
        def _():
            main[pl.ds(HALO + tp, HALO)] = jnp.zeros((HALO, ch, tq), BF16)

        @pl.when(up)
        def _():
            last.wait_recv()

        @pl.when(jnp.logical_not(up))
        def _():
            main[pl.ds(0, HALO)] = jnp.zeros((HALO, ch, tq), BF16)

        lax.fori_loop(0, 2, pack, 0)
        begin(1)
        lax.fori_loop(blocks - 2, blocks, pack, 0)
        begin(2)

        for n in range(3):
            @pl.when(right)
            def _(n=n):
                side(0, n).wait_recv()

            @pl.when(left)
            def _(n=n):
                side(1, n).wait_recv()

        for s, there in ((0, right), (1, left)):
            @pl.when(jnp.logical_not(there))
            def _(s=s):
                pack_in[which, s] = jnp.zeros(pack_in.shape[2:], BF16)

        def unpack(b, carry):
            after = pack_in[which, 0, b]
            before = pack_in[which, 1, b]
            for j in range(PER):
                a = pltpu.roll(after, (-HALO * j) % tq, 1) if j else after
                z = pltpu.roll(before, (-HALO * (j + 1)) % tq, 1)
                halo[b * PER + j] = jnp.where(low, a, z)
            return carry

        lax.fori_loop(0, blocks, unpack, 0)

        def finish():
            @pl.when(up)
            def _():
                first.wait_send()

            @pl.when(down)
            def _():
                last.wait_send()

            for n in range(3):
                @pl.when(left)
                def _(n=n):
                    side(0, n).wait_send()

                @pl.when(right)
                def _(n=n):
                    side(1, n).wait_send()

        return finish

    def taps(main, halo, d, wide):
        lm, lh = pltpu.roll(main, tq - d, 1), pltpu.roll(halo, tq - d, 1)
        rm, rh = pltpu.roll(main, d, 1), pltpu.roll(halo, d, 1)
        head, tail = lane < d, lane >= tq - d
        first = [jnp.where(head, rh, rm), main, jnp.where(tail, lh, lm)]
        first = jnp.concatenate(first, axis=0)
        if not wide:
            return first
        second = [jnp.where(head, rm, rh), halo, jnp.where(tail, lm, lh)]
        return jnp.concatenate([first, jnp.concatenate(second, axis=0)], axis=1)

    def conv(weights, patches, count, lag, done):
        w = weights[...]

        unroll = 4

        def body(b, finish):
            ys = []
            for n in range(unroll):
                def older(back, part):
                    k = n - back * lag
                    span = pl.ds(ch * part, ch)
                    if k >= 0:
                        return ys[k][ch * part : ch * (part + 1)]
                    return ybufs[k % unroll][b + k // unroll, span]

                j = b * unroll + n
                before = older(2, 0) + older(1, 1) if finish else None
                y = jnp.dot(w, patches(j), preferred_element_type=F32)
                ys.append(y)
                if finish:
                    done(j - 2 * lag, before + y[2 * ch :])
                ybufs[n][b] = y[: 2 * ch]

        start = 2 * lag // unroll
        for b in range(start):
            body(b, False)

        def again(b, carry):
            body(b, True)
            return carry

        lax.fori_loop(start, count // unroll, again, 0)

    def wide_rows(main, halo, d):
        return lambda j: taps(main[j], halo[j], d, True)

    def row_pairs(main, halo, d):
        def patches(j):
            one = taps(main[2 * j], halo[2 * j], d, False)
            two = taps(main[2 * j + 1], halo[2 * j + 1], d, False)
            return jnp.concatenate([one, two], axis=1)

        return patches

    side_ok = jnp.where(low, jnp.where(right, 1.0, 0.0), jnp.where(left, 1.0, 0.0))

    def row_ok(p):
        inside = jnp.logical_and(jnp.logical_or(up, p >= 0), jnp.logical_or(down, p < tp))
        return jnp.where(inside, 1.0, 0.0).astype(F32)

    load.wait()
    pad = blocks * PER - ext
    if pad:
        xm[pl.ds(ext, pad)] = jnp.zeros((pad, ch, tq), BF16)
        dm[pl.ds(ext, pad)] = jnp.zeros((pad, ch, tq), BF16)
    tgt_swap = []

    def enter():
        pl.semaphore_wait(
            barrier, SPREAD - 1 + sum(there.astype(jnp.int32) for there, _ in friends)
        )
        tgt_swap.extend(swap(tgt_out, tgt_in, 16))

    finish_x = edges(xm, xh, 0, 0, enter)
    tgt_arrive, tgt_leave = tgt_swap

    def first_done(o, total):
        ok = row_ok(o - D2)
        for n, (src, dst) in enumerate(((xm, hm), (xh, hh))):
            pre = src[o + D1].astype(F32) + total[:, tq * n : tq * (n + 1)] + bias1
            e = jnp.exp(jnp.minimum(pre, 0.0))
            slope1[o, :, tq * n : tq * (n + 1)] = jnp.where(pre > 0, 1.0, e)
            act = jnp.where(pre > 0, pre, e - 1.0) * ok
            dst[o] = (act * side_ok if n else act).astype(BF16)

    conv(w1, wide_rows(xm, xh, D1), ext, D1, first_done)

    def second_done(m, total):
        for n in range(2):
            o = 2 * m + n
            pre = hm[o + D2].astype(F32) + total[:, tq * n : tq * (n + 1)] + bias2
            e = jnp.exp(jnp.minimum(pre, 0.0))
            slope2[o] = jnp.where(pre > 0, 1.0, e)
            hid[o] = jnp.where(pre > 0, pre, e - 1.0).astype(BF16).astype(F32)

    conv(w2, row_pairs(hm, hh, D2), (tp + 2 * D2) // 2, D2 // 2, second_done)

    def turn(n, carry):
        for k in range(4):
            o = 4 * n + k
            plane = hid[:, o, :]
            plane = jnp.transpose(jnp.concatenate([plane, plane], axis=0))
            for h in range(2):
                a = plane[tp * h : tp * h + half]
                b = plane[tp * h + half : tp * (h + 1)]
                turned[pl.ds(half * h, half), o, :] = jnp.where(low_rows, a, b)
        return carry

    lax.fori_loop(0, ch // 4, turn, 0)

    chunk = half // SPREAD
    spans = [pl.ds(chunk * d, chunk) for d in range(SPREAD)]

    def first_leg(h, d):
        if d == 0:
            return pltpu.make_async_remote_copy(
                src_ref=mir_out.at[h, spans[0]], dst_ref=mir_in.at[mine, spans[0]],
                send_sem=leave_sem.at[h, 0], recv_sem=land_sem.at[mine, 0],
                device_id=partners[h], device_id_type=MESH,
            )
        return pltpu.make_async_remote_copy(
            src_ref=mir_out.at[h, spans[d]], dst_ref=relay.at[d - 1, h],
            send_sem=leave_sem.at[h, d], recv_sem=enter_sem.at[h, d],
            device_id=via[d], device_id_type=MESH,
        )

    def last_leg(h, d):
        return pltpu.make_async_remote_copy(
            src_ref=relay.at[d - 1, h], dst_ref=mir_in.at[mine, spans[d]],
            send_sem=pass_sem.at[h, d], recv_sem=land_sem.at[mine, d],
            device_id=relayed[d][h], device_id_type=MESH,
        )

    def landing(g, d):
        return pltpu.make_async_remote_copy(
            src_ref=mir_out.at[g, spans[d]], dst_ref=mir_in.at[g, spans[d]],
            send_sem=leave_sem.at[g, d], recv_sem=land_sem.at[g, d],
            device_id=relays[d][g], device_id_type=MESH,
        )

    order = [d for d in (1, 3, 2, 0) if d < SPREAD]
    for d in order:
        def settle(j, carry, d=d):
            for h in range(2):
                mir_out[h, chunk * d + j] = turned[half * h + chunk * d + j].astype(BF16)
            return carry

        lax.fori_loop(0, chunk, settle, 0)
        for h in range(2):
            if d:
                first_leg(h, d).start()
            else:
                @pl.when(other[h])
                def _(h=h):
                    first_leg(h, 0).start()

                @pl.when(jnp.logical_not(other[h]))
                def _(h=h):
                    mir_in[h, spans[0]] = mir_out[h, spans[0]]

    for d in order[:-1]:
        for h in range(2):
            first_leg(h, d).wait_recv()

            @pl.when(elsewhere(relayed[d][h]))
            def _(h=h, d=d):
                last_leg(h, d).start()

            @pl.when(jnp.logical_not(elsewhere(relayed[d][h])))
            def _(h=h, d=d):
                mir_in[mine, spans[d]] = relay[d - 1, h]

    def mir_arrive(d):
        for g in range(2):
            @pl.when(elsewhere(relays[d][g]))
            def _(g=g):
                landing(g, d).wait_recv()

    def mir_leave():
        for h in range(2):
            @pl.when(other[h])
            def _(h=h):
                first_leg(h, 0).wait_send()

            for d in range(1, SPREAD):
                first_leg(h, d).wait_send()

                @pl.when(elsewhere(relayed[d][h]))
                def _(h=h, d=d):
                    last_leg(h, d).wait_send()

    tgt_arrive()

    real = hw.shape[0]
    bins = bias_pad.shape[0]
    head_pad[...] = jnp.zeros_like(head_pad)
    head_pad[pl.ds(0, real), pl.ds(0, ch)] = hw[...].astype(F32)
    weight = head_pad[...][:bins, :ch].astype(BF16)
    weight_t = jnp.transpose(head_pad[...])[:ch, :bins].astype(BF16)
    bias_pad[...] = jnp.full_like(bias_pad, -1e30)
    bias_pad[pl.ds(0, real)] = jnp.transpose(jnp.broadcast_to(hb[...], (tq, real)))
    bias = jnp.concatenate([bias_pad[...], bias_pad[...]], axis=1)
    bin_ids = lax.broadcasted_iota(jnp.int32, (bins, 2 * tq), 0).astype(F32)
    low_row = lax.broadcasted_iota(jnp.int32, (1, tq), 1) < tq // 2

    def facing(zero, one, mask):
        first = jnp.where(mask, zero, pltpu.roll(one, tq // 2, 1))
        second = jnp.where(mask, pltpu.roll(zero, tq // 2, 1), one)
        return jnp.concatenate([first, second], axis=1)

    tgt_here[...] = target[...].astype(F32)

    def head(j):
        mirrored = facing(mir_in[0, j].astype(F32), mir_in[1, j].astype(F32), low)
        own = jnp.concatenate([hid[j], hid[j + half]], axis=1)
        symmetric = (own + mirrored).astype(BF16)
        logits = jnp.dot(weight, symmetric, preferred_element_type=F32) + bias
        e = jnp.exp(logits - jnp.max(logits, axis=0, keepdims=True))
        probability = e / jnp.sum(e, axis=0, keepdims=True)
        t_own = jnp.concatenate(
            [tgt_here[pl.ds(j, 1), :], tgt_here[pl.ds(j + half, 1), :]], axis=1
        )
        t_mirror = facing(tgt_in[0, pl.ds(j, 1), :], tgt_in[1, pl.ds(j, 1), :], low_row)
        grad = (probability - (bin_ids == t_own).astype(F32)).astype(BF16).astype(F32)
        grad_mirror = (probability - (bin_ids == t_mirror).astype(F32)).astype(BF16).astype(F32)
        bins_sum = (grad + grad_mirror).astype(BF16)
        back = jnp.dot(weight_t, bins_sum, preferred_element_type=F32)
        for n in range(2):
            o = j + half * n
            dm[HALO + o] = (back[:, tq * n : tq * (n + 1)] * slope2[o]).astype(BF16)

    for d in (order[-1:] + order[:-1]):
        mir_arrive(d)

        def heads(n, carry, d=d):
            for k in range(HEADS):
                head(chunk * d + HEADS * n + k)
            return carry

        lax.fori_loop(0, chunk // HEADS, heads, 0)

    finish_d = edges(dm, dh, 1, 8, lambda: None)

    def second_back(o, total):
        ok = row_ok(o - D1)
        for n, (src, dst) in enumerate(((dm, em), (dh, eh))):
            grad = src[o + D2].astype(F32) + total[:, tq * n : tq * (n + 1)]
            delta = grad * slope1[o + D1, :, tq * n : tq * (n + 1)] * ok
            dst[o] = (delta * side_ok if n else delta).astype(BF16)

    conv(w2t, wide_rows(dm, dh, D2), ext, D2, second_back)

    def first_back(m, total):
        for n in range(2):
            o = 2 * m + n
            out[o] = em[o + D1].astype(F32) + total[:, tq * n : tq * (n + 1)]

    conv(w1t, row_pairs(em, eh, D1), (tp + 2 * D1) // 2, D1 // 2, first_back)

    tgt_leave()
    finish_x()
    mir_leave()
    finish_d()


def local_step(
    rows, cols, pair_features, first_kernel, first_bias, second_kernel, second_bias,
    head_weight, head_bias, target,
):
    ch, tp, tq = pair_features.shape
    ext = tp + 2 * HALO
    blocks = -(-ext // PER)
    vmem = pl.BlockSpec(memory_space=pltpu.VMEM)
    plane = lambda n, dtype=BF16: pltpu.VMEM((n, ch, tq), dtype)
    out = pl.pallas_call(
        functools.partial(kernel, rows, cols),
        out_shape=jax.ShapeDtypeStruct((tp, ch, tq), F32),
        in_specs=[pl.BlockSpec(memory_space=pl.ANY)] + [vmem] * 7,
        out_specs=vmem,
        scratch_shapes=[
            plane(blocks * PER), plane(blocks * PER),
            plane(tp + 2 * D2), plane(tp + 2 * D2),
            plane(blocks * PER), plane(blocks * PER),
            plane(tp + 2 * D1), plane(tp + 2 * D1),
            *[pltpu.VMEM((3 * ch, 3 * ch), BF16)] * 4,
            pltpu.VMEM((tp + 2 * D2, ch, 2 * tq), F32),
            plane(tp, F32), plane(tp, F32), plane(tp, F32),
            pltpu.VMEM((2, 2, blocks, ch, tq), BF16),
            pltpu.VMEM((2, 2, blocks, ch, tq), BF16),
            pltpu.VMEM((2, tp // 2, ch, tq), BF16),
            pltpu.VMEM((2, tp // 2, ch, tq), BF16),
            pltpu.VMEM((SPREAD - 1, 2, tp // 2 // SPREAD, ch, tq), BF16),
            pltpu.VMEM((2, tp // 2, tq), F32),
            pltpu.VMEM((2, tp // 2, tq), F32),
            pltpu.VMEM((tp, tq), F32),
            pltpu.SemaphoreType.DMA((18,)),
            pltpu.SemaphoreType.DMA((18,)),
            pltpu.SemaphoreType.DMA((1,)),
            *[pltpu.SemaphoreType.DMA((2, SPREAD))] * 4,
            pltpu.VMEM((128, 128), F32),
            pltpu.VMEM((-(-head_weight.shape[0] // 8) * 8, tq), F32),
            *[pltpu.VMEM((ext // 4 , 2 * ch, 2 * tq), F32) for n in range(8)],
        ],
        compiler_params=pltpu.CompilerParams(
            collective_id=0, has_side_effects=True, vmem_limit_bytes=60 * 1024 * 1024
        ),
    )(
        jnp.transpose(pair_features, (1, 0, 2)),
        first_kernel, second_kernel, first_bias[None], second_bias[None],
        head_weight, head_bias[None], target,
    )
    return jnp.transpose(out, (1, 0, 2))


def solution(mesh):
    placed = (P(None, "col", "row"), P(), P(), P(), P(), P(), P(), P("col", "row"))
    return jax.shard_map(
        functools.partial(local_step, mesh.shape["row"], mesh.shape["col"]),
        mesh=mesh, in_specs=placed, out_specs=P(None, "col", "row"), check_vma=False,
    )
```

```python
import functools

import jax
import jax.numpy as jnp
from jax import lax
from jax.experimental import pallas as pl
from jax.experimental.pallas import tpu as pltpu
from jax.sharding import PartitionSpec as P

D1 = 4
D2 = 8
HALO = D1 + D2
PER = 128 // HALO
SPREAD = 4
SETS = 2
HEADS = 2
MESH = pl.DeviceIdType.MESH
F32, BF16 = jnp.float32, jnp.bfloat16


def kernel(
    rows, cols, x_hbm, k1, k2, b1, b2, hw, hb, target, out,
    xm, xh, hm, hh, dm, dh, em, eh, w1, w1t, w2, w2t, slope1, slope2, hid, turned,
    pack_out, pack_in, mir_out, mir_in, relay, tgt_out, tgt_in, tgt_here, send, recv, local,
    leave_sem, enter_sem, pass_sem, land_sem, x_in, head_pad, bias_pad, *ybufs,
):
    r, c = lax.axis_index("row"), lax.axis_index("col")
    ch, tp, tq = out.shape
    half = tp // 2
    ext = tp + 2 * HALO
    blocks = pack_in.shape[2]
    up, down, left, right = c > 0, c < cols - 1, r > 0, r < rows - 1
    at_up, at_down = (r, jnp.maximum(c - 1, 0)), (r, jnp.minimum(c + 1, cols - 1))
    at_left, at_right = (jnp.maximum(r - 1, 0), c), (jnp.minimum(r + 1, rows - 1), c)
    partners = [(c // 2, 2 * r), (c // 2, 2 * r + 1)]
    mine = c % 2
    group = rows // SPREAD

    def elsewhere(who):
        return jnp.logical_or(who[0] != r, who[1] != c)

    other = [elsewhere(who) for who in partners]

    def shifted(row, d):
        return (row // group + d) % SPREAD * group + row % group

    via = [(shifted(r, d), c) for d in range(SPREAD)]
    relayed = [[(c // 2, 2 * shifted(r, SPREAD - d) + h) for h in range(2)] for d in range(SPREAD)]
    relays = [[(shifted(c // 2, d), 2 * r + g) for g in range(2)] for d in range(SPREAD)]

    load = pltpu.make_async_copy(x_hbm, x_in, local.at[0])
    load.start()

    barrier = pltpu.get_barrier_semaphore()
    friends = [(up, at_up), (down, at_down), (left, at_left), (right, at_right)]
    friends += list(zip(other, partners))
    greeted = friends + [(elsewhere(who), who) for d in range(1, SPREAD) for who in relays[d]]
    friends = friends + [(elsewhere(who), who) for d in range(1, SPREAD) for who in relayed[d]]
    for d in range(1, SPREAD):
        pl.semaphore_signal(barrier, inc=1, device_id=via[d], device_id_type=MESH)
    for there, who in greeted:
        @pl.when(there)
        def _(who=who):
            pl.semaphore_signal(barrier, inc=1, device_id=who, device_id_type=MESH)
    lane = lax.broadcasted_iota(jnp.int32, (ch, tq), 1)
    low = lane < tq // 2

    def remote(src, dst, k, who, k_there=None):
        return pltpu.make_async_remote_copy(
            src_ref=src, dst_ref=dst, send_sem=send.at[k],
            recv_sem=recv.at[k if k_there is None else k_there],
            device_id=who, device_id_type=MESH,
        )

    part = half // SETS

    def outer_first(rows_of_half):
        pieces = [rows_of_half[part * n : part * (n + 1)] for n in range(SETS)]
        return jnp.concatenate(pieces[::-1], axis=0)

    whole = target[...].astype(F32)
    whole = jnp.transpose(jnp.concatenate([whole, whole], axis=0))
    low_rows = lax.broadcasted_iota(jnp.int32, (half, tq), 1) < tq // 2
    for h in range(2):
        a = whole[tp * h : tp * h + half]
        b = outer_first(whole[tp * h + half : tp * (h + 1)])
        tgt_out[h] = jnp.where(low_rows, a, b)
    for kernel_ref, straight, turned_ref in ((k1, w1, w1t), (k2, w2, w2t)):
        for t in range(3):
            blocks_t = [kernel_ref[t, n] for n in range(3)]
            straight[pl.ds(ch * t, ch)] = jnp.concatenate(blocks_t, axis=1)
            back = [jnp.transpose(kernel_ref[2 - t, 2 - n].astype(F32)) for n in range(3)]
            turned_ref[pl.ds(ch * t, ch)] = jnp.concatenate(back, axis=1).astype(BF16)
    bias1 = jnp.transpose(jnp.broadcast_to(b1[...], (tq, ch)))
    bias2 = jnp.transpose(jnp.broadcast_to(b2[...], (tq, ch)))

    def swap(src, dst, k):
        outgoing = [
            remote(src.at[h], dst.at[mine], k + h, partners[h], k + mine) for h in range(2)
        ]
        incoming = [remote(src.at[g], dst.at[g], k + g, partners[g]) for g in range(2)]
        for h in range(2):
            @pl.when(other[h])
            def _(h=h):
                outgoing[h].start()

            @pl.when(jnp.logical_not(other[h]))
            def _(h=h):
                dst[h] = src[h]

        def arrive():
            for g in range(2):
                @pl.when(other[g])
                def _(g=g):
                    incoming[g].wait_recv()

        def leave():
            for h in range(2):
                @pl.when(other[h])
                def _(h=h):
                    outgoing[h].wait_send()

        return arrive, leave

    def edges(main, halo, which, base, parts):
        first = remote(main.at[pl.ds(HALO, HALO)], main.at[pl.ds(HALO + tp, HALO)], base, at_up)
        last = remote(main.at[pl.ds(tp, HALO)], main.at[pl.ds(0, HALO)], base + 1, at_down)

        def side(s, n):
            lo, count = parts[n]
            span = pl.ds(lo, count)
            return remote(
                pack_out.at[which, s, span], pack_in.at[which, s, span],
                base + 2 + 3 * s + n, (at_left, at_right)[s],
            )

        def send_rows():
            @pl.when(up)
            def _():
                first.start()

            @pl.when(down)
            def _():
                last.start()

        def pack(b, carry):
            first_lanes = jnp.zeros((ch, tq), BF16)
            last_lanes = jnp.zeros((ch, tq), BF16)
            for j in range(PER):
                row = main[b * PER + j]
                slot = jnp.logical_and(lane >= HALO * j, lane < HALO * (j + 1))
                moved = pltpu.roll(row, HALO * j, 1) if j else row
                first_lanes = jnp.where(slot, moved, first_lanes)
                last_lanes = jnp.where(slot, pltpu.roll(row, HALO * (j + 1), 1), last_lanes)
            pack_out[which, 0, b] = first_lanes
            pack_out[which, 1, b] = last_lanes
            return carry

        def fill(n):
            lax.fori_loop(parts[n][0], sum(parts[n]), pack, 0)

        def begin(n):
            @pl.when(left)
            def _():
                side(0, n).start()

            @pl.when(right)
            def _():
                side(1, n).start()

        def take_rows():
            @pl.when(down)
            def _():
                first.wait_recv()

            @pl.when(jnp.logical_not(down))
            def _():
                main[pl.ds(HALO + tp, HALO)] = jnp.zeros((HALO, ch, tq), BF16)

            @pl.when(up)
            def _():
                last.wait_recv()

            @pl.when(jnp.logical_not(up))
            def _():
                main[pl.ds(0, HALO)] = jnp.zeros((HALO, ch, tq), BF16)

        def unpack(b, carry):
            after = pack_in[which, 0, b]
            before = pack_in[which, 1, b]
            for j in range(PER):
                a = pltpu.roll(after, (-HALO * j) % tq, 1) if j else after
                z = pltpu.roll(before, (-HALO * (j + 1)) % tq, 1)
                halo[b * PER + j] = jnp.where(low, a, z)
            return carry

        def take(n):
            lo, count = parts[n]
            for s, there in ((0, right), (1, left)):
                @pl.when(there)
                def _(s=s):
                    side(s, n).wait_recv()

                @pl.when(jnp.logical_not(there))
                def _(s=s):
                    pack_in[which, s, pl.ds(lo, count)] = jnp.zeros((count, ch, tq), BF16)

            lax.fori_loop(lo, lo + count, unpack, 0)

        def finish():
            @pl.when(up)
            def _():
                first.wait_send()

            @pl.when(down)
            def _():
                last.wait_send()

            for n in range(3):
                @pl.when(left)
                def _(n=n):
                    side(0, n).wait_send()

                @pl.when(right)
                def _(n=n):
                    side(1, n).wait_send()

        return send_rows, fill, begin, take_rows, take, finish

    def taps(main, halo, d, wide):
        lm, lh = pltpu.roll(main, tq - d, 1), pltpu.roll(halo, tq - d, 1)
        rm, rh = pltpu.roll(main, d, 1), pltpu.roll(halo, d, 1)
        head, tail = lane < d, lane >= tq - d
        first = [jnp.where(head, rh, rm), main, jnp.where(tail, lh, lm)]
        first = jnp.concatenate(first, axis=0)
        if not wide:
            return first
        second = [jnp.where(head, rm, rh), halo, jnp.where(tail, lm, lh)]
        return jnp.concatenate([first, jnp.concatenate(second, axis=0)], axis=1)

    def conv(weights, patches, lag, done, *ranges):
        w = weights[...]

        unroll = 4

        def body(b, finish):
            ys = []
            for n in range(unroll):
                def older(back, part):
                    k = n - back * lag
                    span = pl.ds(ch * part, ch)
                    if k >= 0:
                        return ys[k][ch * part : ch * (part + 1)]
                    return ybufs[k % unroll][b + k // unroll, span]

                j = b * unroll + n
                before = older(2, 0) + older(1, 1) if finish else None
                y = jnp.dot(w, patches(j), preferred_element_type=F32)
                ys.append(y)
                if finish:
                    done(j - 2 * lag, before + y[2 * ch :])
                ybufs[n][b] = y[: 2 * ch]

        def again(b, carry):
            body(b, True)
            return carry

        start = 2 * lag // unroll
        for before_span, lo, hi in ranges:
            before_span()
            for b in range(lo // unroll, lo // unroll + start):
                body(b, False)
            lax.fori_loop(lo // unroll + start, hi // unroll, again, 0)

    def wide_rows(main, halo, d):
        return lambda j: taps(main[j], halo[j], d, True)

    def row_pairs(main, halo, d):
        def patches(j):
            one = taps(main[2 * j], halo[2 * j], d, False)
            two = taps(main[2 * j + 1], halo[2 * j + 1], d, False)
            return jnp.concatenate([one, two], axis=1)

        return patches

    side_ok = jnp.where(low, jnp.where(right, 1.0, 0.0), jnp.where(left, 1.0, 0.0))

    def row_ok(p):
        inside = jnp.logical_and(jnp.logical_or(up, p >= 0), jnp.logical_or(down, p < tp))
        return jnp.where(inside, 1.0, 0.0).astype(F32)

    load.wait()

    def spread(n, carry):
        for k in range(4):
            hid[:, 4 * n + k, :] = x_in[4 * n + k].astype(F32)
        return carry

    def gather(n, carry):
        for k in range(4):
            xm[HALO + 4 * n + k] = hid[4 * n + k].astype(BF16)
        return carry

    lax.fori_loop(0, ch // 4, spread, 0)
    lax.fori_loop(0, tp // 4, gather, 0)
    pad = blocks * PER - ext
    if pad:
        xm[pl.ds(ext, pad)] = jnp.zeros((pad, ch, tq), BF16)
        dm[pl.ds(ext, pad)] = jnp.zeros((pad, ch, tq), BF16)
    send_rows, fill, begin, take_rows, take, finish_x = edges(
        xm, xh, 0, 0, [(2, blocks - 4), (0, 2), (blocks - 2, 2)]
    )
    fill(0)
    pl.semaphore_wait(
        barrier, SPREAD - 1 + sum(there.astype(jnp.int32) for there, _ in friends)
    )
    send_rows()
    begin(0)
    tgt_arrive, tgt_leave = swap(tgt_out, tgt_in, 16)
    take_rows()
    for n in (1, 2):
        fill(n)
        begin(n)

    def corners():
        take(1)
        take(2)

    nothing = lambda: None
    inner, outer = 2 * PER, (blocks - 2) * PER // 4 * 4

    def first_done(o, total):
        ok = row_ok(o - D2)
        for n, (src, dst) in enumerate(((xm, hm), (xh, hh))):
            pre = src[o + D1].astype(F32) + total[:, tq * n : tq * (n + 1)] + bias1
            e = jnp.exp(jnp.minimum(pre, 0.0))
            slope1[o, :, tq * n : tq * (n + 1)] = jnp.where(pre > 0, 1.0, e)
            act = jnp.where(pre > 0, pre, e - 1.0) * ok
            dst[o] = (act * side_ok if n else act).astype(BF16)

    conv(
        w1, wide_rows(xm, xh, D1), D1, first_done,
        (lambda: take(0), inner, outer), (corners, 0, inner + 2 * D1),
        (nothing, outer - 2 * D1, ext),
    )

    def second_done(m, total):
        for n in range(2):
            o = 2 * m + n
            pre = hm[o + D2].astype(F32) + total[:, tq * n : tq * (n + 1)] + bias2
            e = jnp.exp(jnp.minimum(pre, 0.0))
            slope2[o] = jnp.where(pre > 0, 1.0, e)
            hid[o] = jnp.where(pre > 0, pre, e - 1.0).astype(BF16).astype(F32)

    conv(w2, row_pairs(hm, hh, D2), D2 // 2, second_done, (nothing, 0, (tp + 2 * D2) // 2))

    def turn(n, carry):
        for k in range(4):
            o = 4 * n + k
            plane = hid[:, o, :]
            plane = jnp.transpose(jnp.concatenate([plane, plane], axis=0))
            for h in range(2):
                a = plane[tp * h : tp * h + half]
                b = outer_first(plane[tp * h + half : tp * (h + 1)])
                turned[pl.ds(half * h, half), o, :] = jnp.where(low_rows, a, b)
        return carry

    lax.fori_loop(0, ch // 4, turn, 0)

    chunk = part // SPREAD

    def span(s, d):
        return pl.ds(part * s + chunk * d, chunk)

    def travel(src, dst, leaves, lands, who):
        return pltpu.make_async_remote_copy(
            src_ref=src, dst_ref=dst, send_sem=leaves, recv_sem=lands,
            device_id=who, device_id_type=MESH,
        )

    def direct(h, s):
        return travel(
            mir_out.at[h, span(s, 0)], mir_in.at[mine, span(s, 0)],
            leave_sem.at[s, h, 0], land_sem.at[s, mine, 0], partners[h],
        )

    def first_leg(h, s, d):
        return travel(
            mir_out.at[h, span(s, d)], relay.at[s, d - 1, h],
            leave_sem.at[s, h, d], enter_sem.at[s, h, d], via[d],
        )

    def last_leg(h, s, d):
        return travel(
            relay.at[s, d - 1, h], mir_in.at[mine, span(s, d)],
            pass_sem.at[s, h, d], land_sem.at[s, mine, d], relayed[d][h],
        )

    def landing(g, s, d):
        return travel(
            mir_out.at[g, span(s, d)], mir_in.at[g, span(s, d)],
            leave_sem.at[s, g, d], land_sem.at[s, g, d], relays[d][g],
        )

    def depart(s, d):
        def settle(j, carry):
            for h in range(2):
                k = part * s + chunk * d + j
                mir_out[h, k] = turned[half * h + k].astype(BF16)
            return carry

        lax.fori_loop(0, chunk, settle, 0)
        for h in range(2):
            if d:
                first_leg(h, s, d).start()
            else:
                @pl.when(other[h])
                def _(h=h):
                    direct(h, s).start()

                @pl.when(jnp.logical_not(other[h]))
                def _(h=h):
                    mir_in[h, span(s, 0)] = mir_out[h, span(s, 0)]

    def forward(s, d):
        for h in range(2):
            first_leg(h, s, d).wait_recv()

            @pl.when(elsewhere(relayed[d][h]))
            def _(h=h):
                last_leg(h, s, d).start()

            @pl.when(jnp.logical_not(elsewhere(relayed[d][h])))
            def _(h=h):
                mir_in[mine, span(s, d)] = relay[s, d - 1, h]

    order = (1, 3, 2)
    for d in order:
        depart(0, d)
    depart(0, 0)
    for s in range(SETS):
        if s + 1 < SETS:
            for d in order:
                depart(s + 1, d)
        for d in order:
            forward(s, d)
        if s + 1 < SETS:
            depart(s + 1, 0)

    def mir_arrive(s, d):
        for g in range(2):
            @pl.when(elsewhere(relays[d][g]))
            def _(g=g):
                landing(g, s, d).wait_recv()

    def mir_leave():
        for s in range(SETS):
            for h in range(2):
                @pl.when(other[h])
                def _(h=h, s=s):
                    direct(h, s).wait_send()

                for d in order:
                    first_leg(h, s, d).wait_send()

                    @pl.when(elsewhere(relayed[d][h]))
                    def _(h=h, s=s, d=d):
                        last_leg(h, s, d).wait_send()

    tgt_arrive()

    real = hw.shape[0]
    bins = bias_pad.shape[0]
    head_pad[...] = jnp.zeros_like(head_pad)
    head_pad[pl.ds(0, real), pl.ds(0, ch)] = hw[...].astype(F32)
    weight = head_pad[...][:bins, :ch].astype(BF16)
    weight_t = jnp.transpose(head_pad[...])[:ch, :bins].astype(BF16)
    bias_pad[...] = jnp.full_like(bias_pad, -1e30)
    bias_pad[pl.ds(0, real)] = jnp.transpose(jnp.broadcast_to(hb[...], (tq, real)))
    bias = jnp.concatenate([bias_pad[...], bias_pad[...]], axis=1)
    bin_ids = lax.broadcasted_iota(jnp.int32, (bins, 2 * tq), 0).astype(F32)
    low_row = lax.broadcasted_iota(jnp.int32, (1, tq), 1) < tq // 2

    def facing(zero, one, mask):
        first = jnp.where(mask, zero, pltpu.roll(one, tq // 2, 1))
        second = jnp.where(mask, pltpu.roll(zero, tq // 2, 1), one)
        return jnp.concatenate([first, second], axis=1)

    tgt_here[...] = target[...].astype(F32)

    def head(j, apart):
        mirrored = facing(mir_in[0, j].astype(F32), mir_in[1, j].astype(F32), low)
        own = jnp.concatenate([hid[j], hid[j + apart]], axis=1)
        symmetric = (own + mirrored).astype(BF16)
        logits = jnp.dot(weight, symmetric, preferred_element_type=F32) + bias
        e = jnp.exp(logits - jnp.max(logits, axis=0, keepdims=True))
        probability = e / jnp.sum(e, axis=0, keepdims=True)
        t_own = jnp.concatenate(
            [tgt_here[pl.ds(j, 1), :], tgt_here[pl.ds(j + apart, 1), :]], axis=1
        )
        t_mirror = facing(tgt_in[0, pl.ds(j, 1), :], tgt_in[1, pl.ds(j, 1), :], low_row)
        grad = (probability - (bin_ids == t_own).astype(F32)).astype(BF16).astype(F32)
        grad_mirror = (probability - (bin_ids == t_mirror).astype(F32)).astype(BF16).astype(F32)
        bins_sum = (grad + grad_mirror).astype(BF16)
        back = jnp.dot(weight_t, bins_sum, preferred_element_type=F32)
        for n in range(2):
            o = j + apart * n
            dm[HALO + o] = (back[:, tq * n : tq * (n + 1)] * slope2[o]).astype(BF16)

    send_rows, fill, begin, take_rows, take, finish_d = edges(
        dm, dh, 1, 8, [(2, blocks - 5), (0, 2), (blocks - 3, 3)]
    )
    for s in range(SETS):
        apart = tp - part * (2 * s + 1)
        for d in (0, *order):
            mir_arrive(s, d)

            def heads(n, carry, s=s, d=d, apart=apart):
                for k in range(HEADS):
                    head(part * s + chunk * d + HEADS * n + k, apart)
                return carry

            lax.fori_loop(0, chunk // HEADS, heads, 0)
        if s == 0:
            send_rows()
            take_rows()
            for n in (1, 2):
                fill(n)
                begin(n)

    fill(0)
    begin(0)
    for n in (1, 2, 0):
        take(n)

    def second_back(o, total):
        ok = row_ok(o - D1)
        for n, (src, dst) in enumerate(((dm, em), (dh, eh))):
            grad = src[o + D2].astype(F32) + total[:, tq * n : tq * (n + 1)]
            delta = grad * slope1[o + D1, :, tq * n : tq * (n + 1)] * ok
            dst[o] = (delta * side_ok if n else delta).astype(BF16)

    conv(w2t, wide_rows(dm, dh, D2), D2, second_back, (nothing, 0, ext))

    def first_back(m, total):
        for n in range(2):
            o = 2 * m + n
            out[:, o, :] = em[o + D1].astype(F32) + total[:, tq * n : tq * (n + 1)]

    conv(w1t, row_pairs(em, eh, D1), D1 // 2, first_back, (nothing, 0, (tp + 2 * D1) // 2))

    tgt_leave()
    finish_x()
    mir_leave()
    finish_d()


def local_step(
    rows, cols, pair_features, first_kernel, first_bias, second_kernel, second_bias,
    head_weight, head_bias, target,
):
    ch, tp, tq = pair_features.shape
    ext = tp + 2 * HALO
    blocks = -(-ext // PER)
    vmem = pl.BlockSpec(memory_space=pltpu.VMEM)
    plane = lambda n, dtype=BF16: pltpu.VMEM((n, ch, tq), dtype)
    out = pl.pallas_call(
        functools.partial(kernel, rows, cols),
        out_shape=jax.ShapeDtypeStruct((ch, tp, tq), F32),
        in_specs=[pl.BlockSpec(memory_space=pl.ANY)] + [vmem] * 7,
        out_specs=vmem,
        scratch_shapes=[
            plane(blocks * PER), plane(blocks * PER),
            plane(tp + 2 * D2), plane(tp + 2 * D2),
            plane(blocks * PER), plane(blocks * PER),
            plane(tp + 2 * D1), plane(tp + 2 * D1),
            *[pltpu.VMEM((3 * ch, 3 * ch), BF16)] * 4,
            pltpu.VMEM((tp + 2 * D2, ch, 2 * tq), F32),
            plane(tp, F32), plane(tp, F32), plane(tp, F32),
            pltpu.VMEM((2, 2, blocks, ch, tq), BF16),
            pltpu.VMEM((2, 2, blocks, ch, tq), BF16),
            pltpu.VMEM((2, tp // 2, ch, tq), BF16),
            pltpu.VMEM((2, tp // 2, ch, tq), BF16),
            pltpu.VMEM((SETS, SPREAD - 1, 2, tp // 2 // SETS // SPREAD, ch, tq), BF16),
            pltpu.VMEM((2, tp // 2, tq), F32),
            pltpu.VMEM((2, tp // 2, tq), F32),
            pltpu.VMEM((tp, tq), F32),
            pltpu.SemaphoreType.DMA((18,)),
            pltpu.SemaphoreType.DMA((18,)),
            pltpu.SemaphoreType.DMA((1,)),
            *[pltpu.SemaphoreType.DMA((SETS, 2, SPREAD))] * 4,
            pltpu.VMEM((ch, tp, tq), BF16),
            pltpu.VMEM((128, 128), F32),
            pltpu.VMEM((-(-head_weight.shape[0] // 8) * 8, tq), F32),
            *[pltpu.VMEM((ext // 4 , 2 * ch, 2 * tq), F32) for n in range(8)],
        ],
        compiler_params=pltpu.CompilerParams(
            collective_id=0, has_side_effects=True, vmem_limit_bytes=60 * 1024 * 1024
        ),
    )(
        pair_features,
        first_kernel, second_kernel, first_bias[None], second_bias[None],
        head_weight, head_bias[None], target,
    )
    return out


def solution(mesh):
    placed = (P(None, "col", "row"), P(), P(), P(), P(), P(), P(), P("col", "row"))
    return jax.shard_map(
        functools.partial(local_step, mesh.shape["row"], mesh.shape["col"]),
        mesh=mesh, in_specs=placed, out_specs=P(None, "col", "row"), check_vma=False,
    )
```

```python
import functools

import jax
import jax.numpy as jnp
from jax import lax
from jax.experimental import pallas as pl
from jax.experimental.pallas import tpu as pltpu
from jax.sharding import PartitionSpec as P

D1 = 4
D2 = 8
HALO = D1 + D2
PER = 128 // HALO
SPREAD = 4
SETS = 2
UNROLL = 4
HEADS = 2
MESH = pl.DeviceIdType.MESH
F32, BF16 = jnp.float32, jnp.bfloat16


def kernel(
    rows, cols, x_hbm, k1, k2, b1, b2, hw, hb, target, out,
    xm, xh, hm, hh, dm, dh, em, eh, w1, w1t, w2, w2t, slope1, slope2, hid, turned,
    pack_out, pack_in, mir_out, mir_in, relay, tgt_out, tgt_in, tgt_here, send, recv, local,
    leave_sem, enter_sem, pass_sem, land_sem, x_in, head_pad, bias_pad, *ybufs,
):
    r, c = lax.axis_index("row"), lax.axis_index("col")
    ch, tp, tq = out.shape
    half = tp // 2
    ext = tp + 2 * HALO
    blocks = pack_in.shape[2]
    up, down, left, right = c > 0, c < cols - 1, r > 0, r < rows - 1
    at_up, at_down = (r, jnp.maximum(c - 1, 0)), (r, jnp.minimum(c + 1, cols - 1))
    at_left, at_right = (jnp.maximum(r - 1, 0), c), (jnp.minimum(r + 1, rows - 1), c)
    partners = [(c // 2, 2 * r), (c // 2, 2 * r + 1)]
    mine = c % 2
    group = rows // SPREAD

    def elsewhere(who):
        return jnp.logical_or(who[0] != r, who[1] != c)

    other = [elsewhere(who) for who in partners]

    def shifted(row, d):
        return (row // group + d) % SPREAD * group + row % group

    via = [(shifted(r, d), c) for d in range(SPREAD)]
    relayed = [[(c // 2, 2 * shifted(r, SPREAD - d) + h) for h in range(2)] for d in range(SPREAD)]
    relays = [[(shifted(c // 2, d), 2 * r + g) for g in range(2)] for d in range(SPREAD)]

    load = pltpu.make_async_copy(x_hbm, x_in, local.at[0])
    load.start()

    barrier = pltpu.get_barrier_semaphore()
    friends = [(up, at_up), (down, at_down), (left, at_left), (right, at_right)]
    friends += list(zip(other, partners))
    greeted = friends + [(elsewhere(who), who) for d in range(1, SPREAD) for who in relays[d]]
    friends = friends + [(elsewhere(who), who) for d in range(1, SPREAD) for who in relayed[d]]
    for d in range(1, SPREAD):
        pl.semaphore_signal(barrier, inc=1, device_id=via[d], device_id_type=MESH)
    for there, who in greeted:
        @pl.when(there)
        def _(who=who):
            pl.semaphore_signal(barrier, inc=1, device_id=who, device_id_type=MESH)
    lane = lax.broadcasted_iota(jnp.int32, (ch, tq), 1)
    low = lane < tq // 2

    def remote(src, dst, k, who, k_there=None):
        return pltpu.make_async_remote_copy(
            src_ref=src, dst_ref=dst, send_sem=send.at[k],
            recv_sem=recv.at[k if k_there is None else k_there],
            device_id=who, device_id_type=MESH,
        )

    part = half // SETS

    def outer_first(rows_of_half):
        pieces = [rows_of_half[part * n : part * (n + 1)] for n in range(SETS)]
        return jnp.concatenate(pieces[::-1], axis=0)

    whole = target[...].astype(F32)
    whole = jnp.transpose(jnp.concatenate([whole, whole], axis=0))
    low_rows = lax.broadcasted_iota(jnp.int32, (half, tq), 1) < tq // 2
    for h in range(2):
        a = whole[tp * h : tp * h + half]
        b = outer_first(whole[tp * h + half : tp * (h + 1)])
        tgt_out[h] = jnp.where(low_rows, a, b)
    for kernel_ref, straight, turned_ref in ((k1, w1, w1t), (k2, w2, w2t)):
        for t in range(3):
            blocks_t = [kernel_ref[t, n] for n in range(3)]
            straight[pl.ds(ch * t, ch)] = jnp.concatenate(blocks_t, axis=1)
            back = [jnp.transpose(kernel_ref[2 - t, 2 - n].astype(F32)) for n in range(3)]
            turned_ref[pl.ds(ch * t, ch)] = jnp.concatenate(back, axis=1).astype(BF16)
    bias1 = jnp.transpose(jnp.broadcast_to(b1[...], (tq, ch)))
    bias2 = jnp.transpose(jnp.broadcast_to(b2[...], (tq, ch)))

    def swap(src, dst, k):
        outgoing = [
            remote(src.at[h], dst.at[mine], k + h, partners[h], k + mine) for h in range(2)
        ]
        incoming = [remote(src.at[g], dst.at[g], k + g, partners[g]) for g in range(2)]
        for h in range(2):
            @pl.when(other[h])
            def _(h=h):
                outgoing[h].start()

            @pl.when(jnp.logical_not(other[h]))
            def _(h=h):
                dst[h] = src[h]

        def arrive():
            for g in range(2):
                @pl.when(other[g])
                def _(g=g):
                    incoming[g].wait_recv()

        def leave():
            for h in range(2):
                @pl.when(other[h])
                def _(h=h):
                    outgoing[h].wait_send()

        return arrive, leave

    def edges(main, halo, which, base, parts):
        first = remote(main.at[pl.ds(HALO, HALO)], main.at[pl.ds(HALO + tp, HALO)], base, at_up)
        last = remote(main.at[pl.ds(tp, HALO)], main.at[pl.ds(0, HALO)], base + 1, at_down)

        def side(s, n):
            lo, count = parts[n]
            span = pl.ds(lo, count)
            return remote(
                pack_out.at[which, s, span], pack_in.at[which, s, span],
                base + 2 + 3 * s + n, (at_left, at_right)[s],
            )

        def send_rows():
            @pl.when(up)
            def _():
                first.start()

            @pl.when(down)
            def _():
                last.start()

        def pack(b, carry):
            first_lanes = jnp.zeros((ch, tq), BF16)
            last_lanes = jnp.zeros((ch, tq), BF16)
            for j in range(PER):
                row = main[b * PER + j]
                slot = jnp.logical_and(lane >= HALO * j, lane < HALO * (j + 1))
                moved = pltpu.roll(row, HALO * j, 1) if j else row
                first_lanes = jnp.where(slot, moved, first_lanes)
                last_lanes = jnp.where(slot, pltpu.roll(row, HALO * (j + 1), 1), last_lanes)
            pack_out[which, 0, b] = first_lanes
            pack_out[which, 1, b] = last_lanes
            return carry

        def fill(n):
            lax.fori_loop(parts[n][0], sum(parts[n]), pack, 0)

        def begin(n):
            @pl.when(left)
            def _():
                side(0, n).start()

            @pl.when(right)
            def _():
                side(1, n).start()

        def take_rows():
            @pl.when(down)
            def _():
                first.wait_recv()

            @pl.when(jnp.logical_not(down))
            def _():
                main[pl.ds(HALO + tp, HALO)] = jnp.zeros((HALO, ch, tq), BF16)

            @pl.when(up)
            def _():
                last.wait_recv()

            @pl.when(jnp.logical_not(up))
            def _():
                main[pl.ds(0, HALO)] = jnp.zeros((HALO, ch, tq), BF16)

        def unpack(b, carry):
            after = pack_in[which, 0, b]
            before = pack_in[which, 1, b]
            for j in range(PER):
                a = pltpu.roll(after, (-HALO * j) % tq, 1) if j else after
                z = pltpu.roll(before, (-HALO * (j + 1)) % tq, 1)
                halo[b * PER + j] = jnp.where(low, a, z)
            return carry

        def take(n):
            lo, count = parts[n]
            for s, there in ((0, right), (1, left)):
                @pl.when(there)
                def _(s=s):
                    side(s, n).wait_recv()

                @pl.when(jnp.logical_not(there))
                def _(s=s):
                    pack_in[which, s, pl.ds(lo, count)] = jnp.zeros((count, ch, tq), BF16)

            lax.fori_loop(lo, lo + count, unpack, 0)

        def finish():
            @pl.when(up)
            def _():
                first.wait_send()

            @pl.when(down)
            def _():
                last.wait_send()

            for n in range(3):
                @pl.when(left)
                def _(n=n):
                    side(0, n).wait_send()

                @pl.when(right)
                def _(n=n):
                    side(1, n).wait_send()

        return send_rows, fill, begin, take_rows, take, finish

    def taps(main, halo, d, wide):
        lm, lh = pltpu.roll(main, tq - d, 1), pltpu.roll(halo, tq - d, 1)
        rm, rh = pltpu.roll(main, d, 1), pltpu.roll(halo, d, 1)
        head, tail = lane < d, lane >= tq - d
        first = [jnp.where(head, rh, rm), main, jnp.where(tail, lh, lm)]
        first = jnp.concatenate(first, axis=0)
        if not wide:
            return first
        second = [jnp.where(head, rm, rh), halo, jnp.where(tail, lm, lh)]
        return jnp.concatenate([first, jnp.concatenate(second, axis=0)], axis=1)

    def conv(weights, patches, lag, done, *ranges):
        w = weights[...]

        unroll = UNROLL

        def body(b, finish):
            ys = []
            for n in range(unroll):
                def older(back, part):
                    k = n - back * lag
                    span = pl.ds(ch * part, ch)
                    if k >= 0:
                        return ys[k][ch * part : ch * (part + 1)]
                    return ybufs[k % unroll][b + k // unroll, span]

                j = b * unroll + n
                before = older(2, 0) + older(1, 1) if finish else None
                y = jnp.dot(w, patches(j), preferred_element_type=F32)
                ys.append(y)
                if finish:
                    done(j - 2 * lag, before + y[2 * ch :])
                ybufs[n][b] = y[: 2 * ch]

        def again(b, carry):
            body(b, True)
            return carry

        start = 2 * lag // unroll
        for before_span, lo, hi in ranges:
            before_span()
            for b in range(lo // unroll, lo // unroll + start):
                body(b, False)
            lax.fori_loop(lo // unroll + start, hi // unroll, again, 0)

    def wide_rows(main, halo, d):
        return lambda j: taps(main[j], halo[j], d, True)

    def row_pairs(main, halo, d):
        def patches(j):
            one = taps(main[2 * j], halo[2 * j], d, False)
            two = taps(main[2 * j + 1], halo[2 * j + 1], d, False)
            return jnp.concatenate([one, two], axis=1)

        return patches

    side_ok = jnp.where(low, jnp.where(right, 1.0, 0.0), jnp.where(left, 1.0, 0.0))

    def row_ok(p):
        inside = jnp.logical_and(jnp.logical_or(up, p >= 0), jnp.logical_or(down, p < tp))
        return jnp.where(inside, 1.0, 0.0).astype(F32)

    load.wait()

    def spread(n, carry):
        for k in range(4):
            hid[:, 4 * n + k, :] = x_in[4 * n + k].astype(F32)
        return carry

    def gather(n, carry):
        for k in range(4):
            xm[HALO + 4 * n + k] = hid[4 * n + k].astype(BF16)
        return carry

    lax.fori_loop(0, ch // 4, spread, 0)
    lax.fori_loop(0, tp // 4, gather, 0)
    pad = blocks * PER - ext
    if pad:
        xm[pl.ds(ext, pad)] = jnp.zeros((pad, ch, tq), BF16)
        dm[pl.ds(ext, pad)] = jnp.zeros((pad, ch, tq), BF16)
    send_rows, fill, begin, take_rows, take, finish_x = edges(
        xm, xh, 0, 0, [(2, blocks - 4), (0, 2), (blocks - 2, 2)]
    )
    fill(0)
    pl.semaphore_wait(
        barrier, SPREAD - 1 + sum(there.astype(jnp.int32) for there, _ in friends)
    )
    send_rows()
    begin(0)
    tgt_arrive, tgt_leave = swap(tgt_out, tgt_in, 16)
    take_rows()
    for n in (1, 2):
        fill(n)
        begin(n)

    def corners():
        take(1)
        take(2)

    nothing = lambda: None
    inner, outer = 2 * PER, (blocks - 2) * PER // 4 * 4

    def first_done(o, total):
        ok = row_ok(o - D2)
        for n, (src, dst) in enumerate(((xm, hm), (xh, hh))):
            pre = src[o + D1].astype(F32) + total[:, tq * n : tq * (n + 1)] + bias1
            e = jnp.exp(jnp.minimum(pre, 0.0))
            slope1[o, :, tq * n : tq * (n + 1)] = jnp.where(pre > 0, 1.0, e)
            act = jnp.where(pre > 0, pre, e - 1.0) * ok
            dst[o] = (act * side_ok if n else act).astype(BF16)

    conv(
        w1, wide_rows(xm, xh, D1), D1, first_done,
        (lambda: take(0), inner, outer), (corners, 0, inner + 2 * D1),
        (nothing, outer - 2 * D1, ext),
    )

    def second_done(m, total):
        for n in range(2):
            o = 2 * m + n
            pre = hm[o + D2].astype(F32) + total[:, tq * n : tq * (n + 1)] + bias2
            e = jnp.exp(jnp.minimum(pre, 0.0))
            slope2[o] = jnp.where(pre > 0, 1.0, e)
            hid[o] = jnp.where(pre > 0, pre, e - 1.0).astype(BF16).astype(F32)

    conv(w2, row_pairs(hm, hh, D2), D2 // 2, second_done, (nothing, 0, (tp + 2 * D2) // 2))

    def turn(n, carry):
        for k in range(4):
            o = 4 * n + k
            plane = hid[:, o, :]
            plane = jnp.transpose(jnp.concatenate([plane, plane], axis=0))
            for h in range(2):
                a = plane[tp * h : tp * h + half]
                b = outer_first(plane[tp * h + half : tp * (h + 1)])
                turned[pl.ds(half * h, half), o, :] = jnp.where(low_rows, a, b)
        return carry

    lax.fori_loop(0, ch // 4, turn, 0)

    chunk = part // SPREAD

    def span(s, d):
        return pl.ds(part * s + chunk * d, chunk)

    def travel(src, dst, leaves, lands, who):
        return pltpu.make_async_remote_copy(
            src_ref=src, dst_ref=dst, send_sem=leaves, recv_sem=lands,
            device_id=who, device_id_type=MESH,
        )

    def direct(h, s):
        return travel(
            mir_out.at[h, span(s, 0)], mir_in.at[mine, span(s, 0)],
            leave_sem.at[s, h, 0], land_sem.at[s, mine, 0], partners[h],
        )

    def first_leg(h, s, d):
        return travel(
            mir_out.at[h, span(s, d)], relay.at[s, d - 1, h],
            leave_sem.at[s, h, d], enter_sem.at[s, h, d], via[d],
        )

    def last_leg(h, s, d):
        return travel(
            relay.at[s, d - 1, h], mir_in.at[mine, span(s, d)],
            pass_sem.at[s, h, d], land_sem.at[s, mine, d], relayed[d][h],
        )

    def landing(g, s, d):
        return travel(
            mir_out.at[g, span(s, d)], mir_in.at[g, span(s, d)],
            leave_sem.at[s, g, d], land_sem.at[s, g, d], relays[d][g],
        )

    def depart(s, d):
        def settle(j, carry):
            for h in range(2):
                k = part * s + chunk * d + j
                mir_out[h, k] = turned[half * h + k].astype(BF16)
            return carry

        lax.fori_loop(0, chunk, settle, 0)
        for h in range(2):
            if d:
                first_leg(h, s, d).start()
            else:
                @pl.when(other[h])
                def _(h=h):
                    direct(h, s).start()

                @pl.when(jnp.logical_not(other[h]))
                def _(h=h):
                    mir_in[h, span(s, 0)] = mir_out[h, span(s, 0)]

    def forward(s, d):
        for h in range(2):
            first_leg(h, s, d).wait_recv()

            @pl.when(elsewhere(relayed[d][h]))
            def _(h=h):
                last_leg(h, s, d).start()

            @pl.when(jnp.logical_not(elsewhere(relayed[d][h])))
            def _(h=h):
                mir_in[mine, span(s, d)] = relay[s, d - 1, h]

    order = (1, 3, 2)
    for d in order:
        depart(0, d)
    depart(0, 0)
    for s in range(SETS):
        if s + 1 < SETS:
            for d in order:
                depart(s + 1, d)
        for d in order:
            forward(s, d)
        if s + 1 < SETS:
            depart(s + 1, 0)

    def mir_arrive(s, d):
        for g in range(2):
            @pl.when(elsewhere(relays[d][g]))
            def _(g=g):
                landing(g, s, d).wait_recv()

    def mir_leave():
        for s in range(SETS):
            for h in range(2):
                @pl.when(other[h])
                def _(h=h, s=s):
                    direct(h, s).wait_send()

                for d in order:
                    first_leg(h, s, d).wait_send()

                    @pl.when(elsewhere(relayed[d][h]))
                    def _(h=h, s=s, d=d):
                        last_leg(h, s, d).wait_send()

    tgt_arrive()

    real = hw.shape[0]
    bins = bias_pad.shape[0]
    head_pad[...] = jnp.zeros_like(head_pad)
    head_pad[pl.ds(0, real), pl.ds(0, ch)] = hw[...].astype(F32)
    weight = head_pad[...][:bins, :ch].astype(BF16)
    weight_t = jnp.transpose(head_pad[...])[:ch, :bins].astype(BF16)
    bias_pad[...] = jnp.full_like(bias_pad, -1e30)
    bias_pad[pl.ds(0, real)] = jnp.transpose(jnp.broadcast_to(hb[...], (tq, real)))
    bias = jnp.concatenate([bias_pad[...], bias_pad[...]], axis=1)
    bin_ids = lax.broadcasted_iota(jnp.int32, (bins, 2 * tq), 0).astype(F32)
    low_row = lax.broadcasted_iota(jnp.int32, (1, tq), 1) < tq // 2

    def facing(zero, one, mask):
        first = jnp.where(mask, zero, pltpu.roll(one, tq // 2, 1))
        second = jnp.where(mask, pltpu.roll(zero, tq // 2, 1), one)
        return jnp.concatenate([first, second], axis=1)

    tgt_here[...] = target[...].astype(F32)

    def head(j, apart):
        mirrored = facing(mir_in[0, j].astype(F32), mir_in[1, j].astype(F32), low)
        own = jnp.concatenate([hid[j], hid[j + apart]], axis=1)
        symmetric = (own + mirrored).astype(BF16)
        logits = jnp.dot(weight, symmetric, preferred_element_type=F32) + bias
        e = jnp.exp(logits - jnp.max(logits, axis=0, keepdims=True))
        probability = e / jnp.sum(e, axis=0, keepdims=True)
        t_own = jnp.concatenate(
            [tgt_here[pl.ds(j, 1), :], tgt_here[pl.ds(j + apart, 1), :]], axis=1
        )
        t_mirror = facing(tgt_in[0, pl.ds(j, 1), :], tgt_in[1, pl.ds(j, 1), :], low_row)
        grad = (probability - (bin_ids == t_own).astype(F32)).astype(BF16).astype(F32)
        grad_mirror = (probability - (bin_ids == t_mirror).astype(F32)).astype(BF16).astype(F32)
        bins_sum = (grad + grad_mirror).astype(BF16)
        back = jnp.dot(weight_t, bins_sum, preferred_element_type=F32)
        for n in range(2):
            o = j + apart * n
            dm[HALO + o] = (back[:, tq * n : tq * (n + 1)] * slope2[o]).astype(BF16)

    send_rows, fill, begin, take_rows, take, finish_d = edges(
        dm, dh, 1, 8, [(2, blocks - 5), (0, 2), (blocks - 3, 3)]
    )
    for s in range(SETS):
        apart = tp - part * (2 * s + 1)
        for d in (0, *order):
            mir_arrive(s, d)

            def heads(n, carry, s=s, d=d, apart=apart):
                for k in range(HEADS):
                    head(part * s + chunk * d + HEADS * n + k, apart)
                return carry

            lax.fori_loop(0, chunk // HEADS, heads, 0)
        if s == 0:
            send_rows()
            take_rows()
            for n in (1, 2):
                fill(n)
                begin(n)

    fill(0)
    begin(0)
    def second_back(o, total):
        ok = row_ok(o - D1)
        for n, (src, dst) in enumerate(((dm, em), (dh, eh))):
            grad = src[o + D2].astype(F32) + total[:, tq * n : tq * (n + 1)]
            delta = grad * slope1[o + D1, :, tq * n : tq * (n + 1)] * ok
            dst[o] = (delta * side_ok if n else delta).astype(BF16)

    inner, outer = 2 * PER, (blocks - 3) * PER
    conv(
        w2t, wide_rows(dm, dh, D2), D2, second_back,
        (corners, 0, inner), (nothing, outer, ext),
        (lambda: take(0), inner - 2 * D2, outer + 2 * D2),
    )

    def first_back(m, total):
        for n in range(2):
            o = 2 * m + n
            out[:, o, :] = em[o + D1].astype(F32) + total[:, tq * n : tq * (n + 1)]

    conv(w1t, row_pairs(em, eh, D1), D1 // 2, first_back, (nothing, 0, (tp + 2 * D1) // 2))

    tgt_leave()
    finish_x()
    mir_leave()
    finish_d()


def local_step(
    rows, cols, pair_features, first_kernel, first_bias, second_kernel, second_bias,
    head_weight, head_bias, target,
):
    ch, tp, tq = pair_features.shape
    ext = tp + 2 * HALO
    blocks = -(-ext // PER)
    vmem = pl.BlockSpec(memory_space=pltpu.VMEM)
    plane = lambda n, dtype=BF16: pltpu.VMEM((n, ch, tq), dtype)
    out = pl.pallas_call(
        functools.partial(kernel, rows, cols),
        out_shape=jax.ShapeDtypeStruct((ch, tp, tq), F32),
        in_specs=[pl.BlockSpec(memory_space=pl.ANY)] + [vmem] * 7,
        out_specs=vmem,
        scratch_shapes=[
            plane(blocks * PER), plane(blocks * PER),
            plane(tp + 2 * D2), plane(tp + 2 * D2),
            plane(blocks * PER), plane(blocks * PER),
            plane(tp + 2 * D1), plane(tp + 2 * D1),
            *[pltpu.VMEM((3 * ch, 3 * ch), BF16)] * 4,
            pltpu.VMEM((tp + 2 * D2, ch, 2 * tq), F32),
            plane(tp, F32), plane(tp, F32), plane(tp, F32),
            pltpu.VMEM((2, 2, blocks, ch, tq), BF16),
            pltpu.VMEM((2, 2, blocks, ch, tq), BF16),
            pltpu.VMEM((2, tp // 2, ch, tq), BF16),
            pltpu.VMEM((2, tp // 2, ch, tq), BF16),
            pltpu.VMEM((SETS, SPREAD - 1, 2, tp // 2 // SETS // SPREAD, ch, tq), BF16),
            pltpu.VMEM((2, tp // 2, tq), F32),
            pltpu.VMEM((2, tp // 2, tq), F32),
            pltpu.VMEM((tp, tq), F32),
            pltpu.SemaphoreType.DMA((18,)),
            pltpu.SemaphoreType.DMA((18,)),
            pltpu.SemaphoreType.DMA((1,)),
            *[pltpu.SemaphoreType.DMA((SETS, 2, SPREAD))] * 4,
            pltpu.VMEM((ch, tp, tq), BF16),
            pltpu.VMEM((128, 128), F32),
            pltpu.VMEM((-(-head_weight.shape[0] // 8) * 8, tq), F32),
            *[pltpu.VMEM((ext // UNROLL, 2 * ch, 2 * tq), F32)] * UNROLL,
        ],
        compiler_params=pltpu.CompilerParams(
            collective_id=0, has_side_effects=True, vmem_limit_bytes=60 * 1024 * 1024
        ),
    )(
        pair_features,
        first_kernel, second_kernel, first_bias[None], second_bias[None],
        head_weight, head_bias[None], target,
    )
    return out


def solution(mesh):
    placed = (P(None, "col", "row"), P(), P(), P(), P(), P(), P(), P("col", "row"))
    return jax.shard_map(
        functools.partial(local_step, mesh.shape["row"], mesh.shape["col"]),
        mesh=mesh, in_specs=placed, out_specs=P(None, "col", "row"), check_vma=False,
    )
```
